128 devices in a mesh: ha: 8 (over z_lo, x), wa: 16 (over z_hi, y, core).
Axes of the slice: x: 4, y: 4, z: 4 (z_hi: 2, z_lo: 2; z = z_hi * 2 + z_lo), core: 2. Of those that a mesh axis runs over, the one named last changes fastest.
Arguments:
- field: bfloat16 [384, 1024, 256], P('ha', 'wa'), may hold values from -41 to 41
- expand_w: bfloat16 [256, 1024], replicated, may hold values from -0.375 to 0.375
- dw_kernel: float32 [9, 1024], replicated, may hold values from -2 to 2
- project_w: bfloat16 [1024, 256], replicated, may hold values from -0.1875 to 0.1875
- blk_qkv: bfloat16 [256, 768], replicated, may hold values from -0.375 to 0.375
- blk_out: bfloat16 [256, 256], replicated, may hold values from -0.375 to 0.375
- blk_table: float32 [225, 8], replicated, may hold values from -4 to 290
- blk_index: int32 [64, 64], replicated, may hold values from 0 to 224, as said below
- blk_up: bfloat16 [256, 1024], replicated, may hold values from -0.375 to 0.375
- blk_down: bfloat16 [1024, 256], replicated, may hold values from -0.1875 to 0.1875
- grid_qkv: bfloat16 [256, 768], replicated, may hold values from -0.375 to 0.375
- grid_out: bfloat16 [256, 256], replicated, may hold values from -0.375 to 0.375
- grid_table: float32 [225, 8], replicated, may hold values from -4 to 290
- grid_index: int32 [64, 64], replicated, may hold values from 0 to 224, as said below
- grid_up: bfloat16 [256, 1024], replicated, may hold values from -0.375 to 0.375
- grid_down: bfloat16 [1024, 256], replicated, may hold values from -0.1875 to 0.1875
Outputs:
- updated: bfloat16 [384, 1024, 256], P('ha', 'wa')
The draws below stay inside these ranges and needn't reach their ends.
Inputs may be any that keep to these rules, and one draw needn't show every extreme that they name: `blk_index`: two entries are equal exactly when their query and key positions differ by the same row and column offsets inside the window. `grid_index`: two entries are equal exactly when their query and key positions differ by the same row and column offsets inside the window.
All inputs are finite; a program needn't handle non-finite values.
Results may differ from the reference program's by a relative error of at most 0.013.
Values may be sent and summed in bfloat16 or wider, within the bound.
No kernel may reach another device: no remote copies, remote signals or barrier semaphores. Data moves between devices by JAX's collectives and lax.ppermute only.
A program may use at most 128 MiB of HBM per device.

```python
import math
import jax
import jax.numpy as jnp
from jax import lax

C = 256
HEADS = 8
EXPAND = 1024
FFN = 1024
BUCKETS = 225
H = 384
W = 1024


def draw_field(key, part):
    base_key = jax.random.fold_in(key, 3)
    first, second, third = jax.random.split(base_key, 3)
    cell_scale = jnp.exp(jax.random.uniform(second, (H, W, 1), minval=-1.15, maxval=1.15))
    channel_scale = jnp.exp(jax.random.uniform(third, (1, 1, C), minval=-1.15, maxval=1.15))
    base = jnp.clip(jax.random.normal(first, (H, W, C)), -4.0, 4.0)
    return (base * cell_scale * channel_scale).astype(jnp.float32).astype(jnp.bfloat16)


def table_draw(key):
    base = jnp.clip(jax.random.normal(key, (BUCKETS, HEADS)), -4.0, 4.0)
    return base.astype(jnp.float32)


def draw_blk_table(key, part):
    return table_draw(jax.random.fold_in(key, 5))


def draw_grid_table(key, part):
    return table_draw(jax.random.fold_in(key, 9))


def index_draw(key):
    order = jax.random.permutation(key, BUCKETS)
    position = jnp.arange(64, dtype=jnp.int32)
    prow = position // 8
    pcol = position % 8
    offsets = (prow[:, None] - prow[None, :] + 7) * 15 + (pcol[:, None] - pcol[None, :] + 7)
    return order[offsets].astype(jnp.int32)


def draw_blk_index(key, part):
    return index_draw(jax.random.fold_in(key, 11))


def draw_grid_index(key, part):
    return index_draw(jax.random.fold_in(key, 13))


def centred(key, extent, scale, reach, kind=jnp.bfloat16):
    return jnp.clip(scale * jax.random.normal(key, extent, jnp.float32), -reach, reach).astype(kind)


def setup_inputs(seed: int = 0) -> dict:
    key_list = jax.random.split(jax.random.key(seed), 17)
    field = draw_field(jax.random.fold_in(key_list[16], 71), 0)
    expand_w = centred(key_list[1], (C, EXPAND), C ** -0.5, 0.375)
    dw_kernel = centred(key_list[2], (9, EXPAND), 9 ** -0.5, 2.0, jnp.float32)
    project_w = centred(key_list[3], (EXPAND, C), EXPAND ** -0.5, 0.1875)
    blk_qkv = centred(key_list[4], (C, 3 * C), C ** -0.5, 0.375)
    blk_out = centred(key_list[5], (C, C), C ** -0.5, 0.375)
    blk_table = draw_blk_table(jax.random.fold_in(key_list[16], 71), 0)
    blk_index = draw_blk_index(jax.random.fold_in(key_list[16], 71), 0)
    blk_up = centred(key_list[8], (C, FFN), C ** -0.5, 0.375)
    blk_down = centred(key_list[9], (FFN, C), FFN ** -0.5, 0.1875)
    grid_qkv = centred(key_list[10], (C, 3 * C), C ** -0.5, 0.375)
    grid_out = centred(key_list[11], (C, C), C ** -0.5, 0.375)
    grid_table = draw_grid_table(jax.random.fold_in(key_list[16], 71), 0)
    grid_index = draw_grid_index(jax.random.fold_in(key_list[16], 71), 0)
    grid_up = centred(key_list[14], (C, FFN), C ** -0.5, 0.375)
    grid_down = centred(key_list[15], (FFN, C), FFN ** -0.5, 0.1875)
    return dict(field=field, expand_w=expand_w, dw_kernel=dw_kernel, project_w=project_w, blk_qkv=blk_qkv, blk_out=blk_out, blk_table=blk_table, blk_index=blk_index, blk_up=blk_up, blk_down=blk_down, grid_qkv=grid_qkv, grid_out=grid_out, grid_table=grid_table, grid_index=grid_index, grid_up=grid_up, grid_down=grid_down)


EPS = 1e-05

def normalize(values):
    wide = values.astype(jnp.float32)
    center = wide - lax.optimization_barrier(jnp.mean(wide, axis=-1, keepdims=True))
    spread = lax.optimization_barrier(jnp.mean(center * center, axis=-1, keepdims=True))
    return (center * lax.rsqrt(spread + EPS)).astype(jnp.bfloat16)

def relative(table, index):
    return jnp.transpose(table[index], (2, 0, 1)).astype(jnp.float32)

def feed_forward(values, up_w, down_w):
    inner = jax.nn.gelu(jnp.dot(normalize(values), up_w, preferred_element_type=jnp.float32)).astype(jnp.bfloat16)
    return (values.astype(jnp.float32) + jnp.dot(inner, down_w, preferred_element_type=jnp.float32)).astype(jnp.bfloat16)

def attention_layer(windows, qkv_w, out_w, bias, up_w, down_w):
    nwin = windows.shape[0]
    flat = windows.reshape(nwin * 64, C)
    qkv = jnp.dot(normalize(flat), qkv_w, preferred_element_type=jnp.float32).astype(jnp.bfloat16)
    qkv = qkv.reshape(nwin, 64, 3, HEADS, C // HEADS).astype(jnp.float32)
    scores = jnp.einsum('wphd,wqhd->whpq', qkv[:, :, 0], qkv[:, :, 1])
    scores = scores / math.sqrt(C // HEADS) + bias[None]
    weights = jax.nn.softmax(scores, axis=-1).astype(jnp.bfloat16).astype(jnp.float32)
    mixed = jnp.einsum('whpq,wqhd->wphd', weights, qkv[:, :, 2]).astype(jnp.bfloat16)
    mixed = mixed.reshape(nwin * 64, C)
    current = (flat.astype(jnp.float32) + jnp.dot(mixed, out_w, preferred_element_type=jnp.float32)).astype(jnp.bfloat16)
    return feed_forward(current, up_w, down_w).reshape(nwin, 64, C)

def reference(field, expand_w, dw_kernel, project_w, blk_qkv, blk_out, blk_table, blk_index, blk_up, blk_down, grid_qkv, grid_out, grid_table, grid_index, grid_up, grid_down):
    normed = normalize(field)
    padded = jnp.pad(normed, ((1, 1), (1, 1), (0, 0)))

    def conv_strip(start):
        rows_in = lax.dynamic_slice_in_dim(padded, start, 10, 0)
        hidden = jax.nn.gelu(jnp.dot(rows_in.reshape(-1, C), expand_w, preferred_element_type=jnp.float32))
        hidden = hidden.astype(jnp.bfloat16).reshape(10, W + 2, EXPAND)
        depth = jnp.zeros((8, W, EXPAND), jnp.float32)
        for row_step in range(3):
            for col_step in range(3):
                depth = depth + dw_kernel[3 * row_step + col_step] * hidden[row_step:row_step + 8, col_step:col_step + W].astype(jnp.float32)
        activated = jax.nn.gelu(depth).astype(jnp.bfloat16)
        return jnp.dot(activated.reshape(-1, EXPAND), project_w, preferred_element_type=jnp.float32).reshape(8, W, C)
    starts = (jnp.arange(H // 8) * 8).astype(jnp.int32)
    branch = lax.map(conv_strip, starts).reshape(H, W, C)
    current = (field.astype(jnp.float32) + branch).astype(jnp.bfloat16)
    blk_bias = relative(blk_table, blk_index)

    def block_strip(strip):
        windows = strip.reshape(8, W // 8, 8, C).transpose(1, 0, 2, 3).reshape(-1, 64, C)
        result = attention_layer(windows, blk_qkv, blk_out, blk_bias, blk_up, blk_down)
        return result.reshape(W // 8, 8, 8, C).transpose(1, 0, 2, 3).reshape(8, W, C)
    current = lax.map(block_strip, current.reshape(H // 8, 8, W, C)).reshape(H, W, C)
    grid_bias = relative(grid_table, grid_index)
    grouped = current.reshape(8, H // 8, W, C).transpose(1, 0, 2, 3)

    def grid_slab(slab):
        windows = slab.reshape(8, 8, W // 8, C).transpose(2, 0, 1, 3).reshape(-1, 64, C)
        result = attention_layer(windows, grid_qkv, grid_out, grid_bias, grid_up, grid_down)
        return result.reshape(W // 8, 8, 8, C).transpose(1, 2, 0, 3).reshape(8, W, C)
    result = lax.map(grid_slab, grouped)
    return result.transpose(1, 0, 2, 3).reshape(H, W, C)
```

```python
import functools
import math

import jax
import jax.numpy as jnp
from jax import lax
from jax.experimental import pallas as pl
from jax.experimental.pallas import tpu as pltpu
from jax.sharding import Mesh
from jax.sharding import PartitionSpec as P

EPS = 1e-05
LOG2E = 1.4426950408889634
C0 = 0.7978845608028654
C1 = C0 * 0.044715
F32 = jnp.float32
BF16 = jnp.bfloat16
WIDE = 80
CHUNKS = (3, 3)
PARAMS = pltpu.CompilerParams(vmem_limit_bytes=56 << 20)


def norm(x):
    center = x - jnp.sum(x, axis=-1, keepdims=True) * (1.0 / 256.0)
    spread = jnp.sum(center * center, axis=-1, keepdims=True) * (1.0 / 256.0)
    return (center * lax.rsqrt(spread + EPS)).astype(BF16)


def gelu2(v):
    v = v.astype(BF16)
    u = v * (jnp.asarray(C1, BF16) * (v * v) + jnp.asarray(C0, BF16))
    return v + v * jnp.tanh(u)


def mm(a, b):
    return jnp.dot(a, b, preferred_element_type=F32)


def mm_nt(a, b):
    return lax.dot_general(a, b, (((1,), (1,)), ((), ())), preferred_element_type=F32)


def make_bias(table_ref, index_ref, bias_ref):
    index = index_ref[...]
    low = lax.broadcasted_iota(jnp.int32, (64, 128), 1) < 64
    upper = index >= 128
    within = jnp.bitwise_and(index, 127)
    got = []
    for h in range(8):
        halves = []
        for half in range(2):
            row = jnp.broadcast_to(table_ref[h : h + 1, 128 * half : 128 * half + 128] * LOG2E, (64, 128))
            halves.append(jnp.take_along_axis(row, within, axis=1))
        got.append(jnp.where(upper, halves[1], halves[0]))
    for h in range(0, 8, 2):
        g, c = h // 4, (h % 4) // 2
        lanes = slice(128 * c, 128 * c + 128)
        bias_ref[g, 0:64, lanes] = jnp.where(low, got[h], got[h + 1])
        bias_ref[g, 64:128, lanes] = jnp.where(low, got[h + 1], got[h])


def attend(windows, n_ref, qkv_ref, wt_ref, bias_ref, k_ref, qvt_ref, s_ref, e_ref, d_ref, o_ref):
    scale = LOG2E / math.sqrt(32.0)
    k_ref[...] = mm(n_ref[...], qkv_ref[:, 256:512]).astype(BF16)
    qvt_ref[...] = mm_nt(wt_ref[...], n_ref[...]).astype(BF16)
    lane = lax.broadcasted_iota(jnp.int32, (1, 128), 1)
    low = lane < 64
    even = (lane // 32) % 2 == 0
    lowm = low.astype(BF16)
    highm = (lane >= 64).astype(BF16)
    units = windows

    def scores(u):
        pair, g = u // 2, u % 2
        cols = slice(128 * g, 128 * g + 128)
        rows = 128 * pair
        qt = qvt_ref[cols, rows : rows + 128]
        turn = pltpu.roll(qt.astype(F32), 64, 1).astype(BF16)
        zero = jnp.zeros((32, 128), BF16)
        for side in range(2):
            straight = qt * (lowm if side == 0 else highm)
            rolled = turn * (highm if side == 0 else lowm)
            blocks = []
            for c in range(2):
                parts = [zero] * 4
                parts[2 * c] = straight[64 * c : 64 * c + 32]
                parts[2 * c + 1] = rolled[64 * c + 32 : 64 * c + 64]
                blocks.append(jnp.concatenate(parts, axis=0))
            keys = k_ref[rows + 64 * side : rows + 64 * side + 64, cols]
            s_ref[u % 2, 64 * side : 64 * side + 64, :] = mm(keys, jnp.concatenate(blocks, axis=1))

    def soften(u):
        g = u % 2
        for side in range(2):
            rows = slice(64 * side, 64 * side + 64)
            for c in range(2):
                lanes = slice(128 * c, 128 * c + 128)
                s = s_ref[u % 2, rows, lanes] * scale + bias_ref[g, rows, lanes]
                e = jnp.exp2(s - jnp.max(s, axis=0, keepdims=True))
                d_ref[u % 2, side : side + 1, lanes] = 1.0 / jnp.sum(e, axis=0, keepdims=True)
                e_ref[u % 2, rows, lanes] = e.astype(BF16)

    def mix(u):
        pair, g = u // 2, u % 2
        vt = qvt_ref[256 + 128 * g : 256 + 128 * g + 128, 128 * pair : 128 * pair + 128]
        r = mm(jnp.concatenate([vt * lowm, vt * highm], axis=0), e_ref[u % 2])
        parts = []
        for j in range(4):
            lanes = slice(128 * (j // 2), 128 * (j // 2) + 128)
            a, b = r[32 * j : 32 * j + 32, lanes], r[128 + 32 * j : 128 + 32 * j + 32, lanes]
            da, db = d_ref[u % 2, 0:1, lanes], d_ref[u % 2, 1:2, lanes]
            if j % 2 == 1:
                a, b, da, db = b, a, db, da
            parts.append(jnp.where(low, a, b) * jnp.where(low, da, db))
        t = jnp.concatenate(parts, axis=0).T
        o = jnp.concatenate(
            [jnp.where(even, t[0:64], t[64:128]), jnp.where(even, t[64:128], t[0:64])], axis=0
        )
        o_ref[128 * pair : 128 * pair + 128, 128 * g : 128 * g + 128] = o.astype(BF16)

    for step in range(units + 2):
        if step >= 2:
            mix(step - 2)
        if step < units:
            scores(step)
        if 1 <= step < units + 1:
            soften(step - 1)


def project_and_feed(x_ref, o_ref, g_ref, n_ref, out_w_ref, up_ref, down_ref, y_ref):
    y = x_ref[...] + mm(o_ref[...], out_w_ref[...])
    x_ref[...] = y
    n_ref[...] = norm(y)
    for p in range(4):
        lanes = slice(256 * p, 256 * p + 256)
        g_ref[:, lanes] = gelu2(mm(n_ref[...], up_ref[:, lanes])).astype(BF16)
    y_ref[...] = x_ref[...] + 0.5 * mm(g_ref[...], down_ref[...])


def local_kernel(
    first, strips,
    x_ref, above_ref, below_ref, left_ref, right_ref,
    ew_ref, dw_ref, pw_ref, qkv_ref, wt_ref, table_ref, index_ref, out_w_ref, up_ref, down_ref,
    res_ref,
    hid_ref, act_ref, xn_ref, bias_ref, xw_ref, n_ref, k_ref, qvt_ref, s_ref, e_ref, d_ref, o_ref, g_ref, y_ref,
):
    rows = 8 * strips
    side = 64 * (rows + 2)
    pad = -(-(rows + 2) // 16) * 16
    last = x_ref.shape[0]
    make_bias(table_ref, index_ref, bias_ref)
    for r in range(rows + 2):
        image = 8 * first + r - 1
        x = above_ref[0] if image < 0 else below_ref[0] if image >= last else x_ref[image]
        xn_ref[64 * r : 64 * r + 64] = norm(x.astype(F32))
    for i, ref in enumerate((left_ref, right_ref)):
        xn_ref[side + pad * i : side + pad * i + rows + 2] = norm(
            ref[8 * first : 8 * first + rows + 2].astype(F32)
        )

    def hidden(p, buf):
        h = gelu2(mm(xn_ref[...], ew_ref[:, pl.ds(256 * p, 256)])).astype(F32)
        for c in range(2):
            lanes = slice(128 * c, 128 * c + 128)
            hid_ref[buf, c, :, 8:72, :] = h[0:side, lanes].reshape(rows + 2, 64, 128)
            for r in range(rows + 2):
                hid_ref[buf, c, r, 7:8, :] = h[side + r : side + r + 1, lanes]
                hid_ref[buf, c, r, 72:73, :] = h[side + pad + r : side + pad + r + 1, lanes]

    def conv(p, buf):
        for strip in range(strips):
            for c in range(2):
                w = (dw_ref[:, pl.ds(256 * p + 128 * c, 128)] * 0.5).astype(BF16)
                for half in range(2):
                    begin = 7 + 32 * half
                    acc = [None] * 8
                    for ir in range(10):
                        h = [
                            hid_ref[buf, c, 8 * strip + ir, begin + d : begin + d + 32, :].astype(BF16)
                            for d in range(3)
                        ]
                        for dy in range(3):
                            orow = ir - dy
                            if 0 <= orow < 8:
                                t = h[0] * w[3 * dy : 3 * dy + 1] + h[1] * w[3 * dy + 1 : 3 * dy + 2]
                                t = t + h[2] * w[3 * dy + 2 : 3 * dy + 3]
                                acc[orow] = t if acc[orow] is None else acc[orow] + t
                        done = ir - 2
                        if done >= 0:
                            to = 64 * (8 * strip + done) + 32 * half
                            act_ref[to : to + 32, 128 * c : 128 * c + 128] = gelu2(acc[done])
            part = slice(512 * strip, 512 * strip + 512)
            y_ref[part] += mm(act_ref[part], pw_ref[pl.ds(256 * p, 256), :])

    y_ref[...] = jnp.zeros_like(y_ref)
    hidden(0, 0)

    def quarter(p, carry):
        hidden(p + 1, (p + 1) % 2)
        conv(p, p % 2)
        return carry

    lax.fori_loop(0, 3, quarter, 0)
    conv(3, 1)

    for strip in range(strips):
        for r in range(8):
            at = 64 * (8 * strip + r)
            x = x_ref[8 * (first + strip) + r].astype(F32) + 0.5 * y_ref[at : at + 64]
            for w in range(8):
                to = 64 * (8 * strip + w) + 8 * r
                xw_ref[to : to + 8] = x[8 * w : 8 * w + 8]
    n_ref[...] = norm(xw_ref[...])
    attend(8 * strips, n_ref, qkv_ref, wt_ref, bias_ref, k_ref, qvt_ref, s_ref, e_ref, d_ref, o_ref)
    project_and_feed(xw_ref, o_ref, g_ref, n_ref, out_w_ref, up_ref, down_ref, y_ref)
    for strip in range(strips):
        for w in range(8):
            at = 64 * (8 * strip + w)
            res_ref[8 * strip : 8 * strip + 8, 8 * w : 8 * w + 8, :] = (
                y_ref[at : at + 64].reshape(8, 8, 256).astype(BF16)
            )


def grid_kernel(
    windows,
    x_ref, qkv_ref, wt_ref, table_ref, index_ref, out_w_ref, up_ref, down_ref,
    res_ref,
    xs_ref, bias_ref, xw_ref, n_ref, k_ref, qvt_ref, s_ref, e_ref, d_ref, o_ref, g_ref, y_ref,
):
    make_bias(table_ref, index_ref, bias_ref)
    x = x_ref[...].astype(F32).reshape(64 * windows, 256)
    xs_ref[0] = x[:, 0:128]
    xs_ref[1] = x[:, 128:256]
    for w in range(windows):
        rows = slice(64 * w, 64 * w + 64)
        for half in range(2):
            xw_ref[rows, 128 * half : 128 * half + 128] = xs_ref[half, pl.ds(w, 64, stride=windows), :]
    n_ref[...] = norm(xw_ref[...])
    attend(windows, n_ref, qkv_ref, wt_ref, bias_ref, k_ref, qvt_ref, s_ref, e_ref, d_ref, o_ref)
    project_and_feed(xw_ref, o_ref, g_ref, n_ref, out_w_ref, up_ref, down_ref, y_ref)
    for w in range(windows):
        rows = slice(64 * w, 64 * w + 64)
        for half in range(2):
            xs_ref[half, pl.ds(w, 64, stride=windows), :] = y_ref[rows, 128 * half : 128 * half + 128]
    y = jnp.concatenate([xs_ref[0], xs_ref[1]], axis=1)
    res_ref[...] = y.reshape(64, windows, 256).astype(BF16)


def attend_scratch(windows):
    rows = 64 * windows
    return [
        pltpu.VMEM((2, 128, 256), F32),
        pltpu.VMEM((rows, 256), F32),
        pltpu.VMEM((rows, 256), BF16),
        pltpu.VMEM((rows, 256), BF16),
        pltpu.VMEM((512, rows), BF16),
        pltpu.VMEM((2, 128, 256), F32),
        pltpu.VMEM((2, 128, 256), BF16),
        pltpu.VMEM((2, 2, 256), F32),
        pltpu.VMEM((rows, 256), BF16),
        pltpu.VMEM((rows, 1024), BF16),
        pltpu.VMEM((rows, 256), F32),
    ]


def in_vmem(count):
    return [pl.BlockSpec(memory_space=pltpu.VMEM)] * count


def local_stage(first, strips, cells, weights):
    ops = tuple(cells) + tuple(weights)
    rows = 8 * strips
    pad = -(-(rows + 2) // 16) * 16
    return pl.pallas_call(
        functools.partial(local_kernel, first, strips),
        in_specs=in_vmem(len(ops)),
        out_specs=in_vmem(1)[0],
        out_shape=jax.ShapeDtypeStruct((rows, 64, 256), BF16),
        scratch_shapes=[
            pltpu.VMEM((2, 2, rows + 2, WIDE, 128), F32),
            pltpu.VMEM((64 * rows, 256), BF16),
            pltpu.VMEM((64 * (rows + 2) + 2 * pad, 256), BF16),
        ]
        + attend_scratch(8 * strips),
        compiler_params=PARAMS,
        name="local_stage",
    )(*ops)


def grid_stage(x, weights):
    windows = x.shape[1]
    ops = (x,) + tuple(weights)
    return pl.pallas_call(
        functools.partial(grid_kernel, windows),
        in_specs=in_vmem(len(ops)),
        out_specs=in_vmem(1)[0],
        out_shape=jax.ShapeDtypeStruct(x.shape, BF16),
        scratch_shapes=[pltpu.VMEM((2, 64 * windows, 128), F32)] + attend_scratch(windows),
        compiler_params=PARAMS,
        name="grid_stage",
    )(*ops)


def bias_operands(table, index):
    turned_index = index.T
    return (
        jnp.pad(table.T, ((0, 0), (0, 256 - table.shape[0]))),
        jnp.concatenate([turned_index, turned_index], axis=1),
    )


def turned(qkv):
    return jnp.concatenate([qkv[:, :256], qkv[:, 512:]], axis=1).T


def neighbours(before, after, axes):
    count = lax.axis_size(axes)
    up = [(i, i + 1) for i in range(count - 1)]
    down = [(j, i) for i, j in up]
    return lax.ppermute(before, axes, up), lax.ppermute(after, axes, down)


def on_device(
    field, expand_w, dw_kernel, project_w,
    blk_qkv, blk_out, blk_table, blk_index, blk_up, blk_down,
    grid_qkv, grid_out, grid_table, grid_index, grid_up, grid_down,
):
    rows, cols, width = field.shape
    above, below = neighbours(field[-1:], field[:1], "ha")
    first = jnp.concatenate([above[:, 0], field[:, 0], below[:, 0]], axis=0)
    final = jnp.concatenate([above[:, -1], field[:, -1], below[:, -1]], axis=0)
    left, right = neighbours(final, first, ("wh", "core"))
    cells = (field, above, below, left, right)
    local_w = (expand_w, dw_kernel, project_w, blk_qkv, turned(blk_qkv))
    local_w += bias_operands(blk_table, blk_index) + (blk_out, blk_up, blk_down)
    grid_w = (grid_qkv, turned(grid_qkv)) + bias_operands(grid_table, grid_index)
    grid_w += (grid_out, grid_up, grid_down)
    outs = []
    start = 0
    for strips in CHUNKS:
        part = local_stage(start, strips, cells, local_w)
        start += strips
        part = part.reshape(64, strips * 8, width)
        moved = lax.all_to_all(part, ("ha", "wh"), 0, 0, tiled=True)
        done = grid_stage(moved, grid_w)
        back = lax.all_to_all(done, ("ha", "wh"), 0, 0, tiled=True)
        outs.append(back.reshape(strips * 8, cols, width))
    return jnp.concatenate(outs, axis=0)


def solution(mesh):
    split = Mesh(mesh.devices.reshape(8, 8, 2), ("ha", "wh", "core"))
    spec = P("ha", ("wh", "core"), None)
    return jax.shard_map(
        on_device, mesh=split, in_specs=(spec,) + (P(),) * 15, out_specs=spec, check_vma=False
    )
```

```python
import functools
import math

import jax
import jax.numpy as jnp
from jax import lax
from jax.experimental import pallas as pl
from jax.experimental.pallas import tpu as pltpu
from jax.sharding import Mesh
from jax.sharding import PartitionSpec as P

EPS = 1e-05
LOG2E = 1.4426950408889634
C0 = 0.7978845608028654
C1 = C0 * 0.044715
F32 = jnp.float32
BF16 = jnp.bfloat16
WIDE = 80
CHUNKS = (6,)
PARAMS = pltpu.CompilerParams(vmem_limit_bytes=56 << 20)


def norm(x):
    center = x - jnp.sum(x, axis=-1, keepdims=True) * (1.0 / 256.0)
    spread = jnp.sum(center * center, axis=-1, keepdims=True) * (1.0 / 256.0)
    return (center * lax.rsqrt(spread + EPS)).astype(BF16)


def gelu2(v):
    v = v.astype(BF16)
    u = v * (jnp.asarray(C1, BF16) * (v * v) + jnp.asarray(C0, BF16))
    return v + v * jnp.tanh(u)


def mm(a, b):
    return jnp.dot(a, b, preferred_element_type=F32)


def mm_nt(a, b):
    return lax.dot_general(a, b, (((1,), (1,)), ((), ())), preferred_element_type=F32)


def make_bias(table_ref, index_ref, bias_ref):
    index = index_ref[...]
    low = lax.broadcasted_iota(jnp.int32, (64, 128), 1) < 64
    upper = index >= 128
    within = jnp.bitwise_and(index, 127)
    got = []
    for h in range(8):
        halves = []
        for half in range(2):
            row = jnp.broadcast_to(table_ref[h : h + 1, 128 * half : 128 * half + 128] * LOG2E, (64, 128))
            halves.append(jnp.take_along_axis(row, within, axis=1))
        got.append(jnp.where(upper, halves[1], halves[0]))
    for h in range(0, 8, 2):
        g, c = h // 4, (h % 4) // 2
        lanes = slice(128 * c, 128 * c + 128)
        bias_ref[g, 0:64, lanes] = jnp.where(low, got[h], got[h + 1])
        bias_ref[g, 64:128, lanes] = jnp.where(low, got[h + 1], got[h])


def attend(windows, n_ref, qkv_ref, wt_ref, bias_ref, k_ref, qvt_ref, o_ref, s_refs, e_refs, d_refs):
    scale = LOG2E / math.sqrt(32.0)
    block = 64 * windows // 2

    def maps(i, carry):
        rows = pl.ds(pl.multiple_of(block * i, 256), block)
        k_ref[rows] = mm(n_ref[rows], qkv_ref[:, 256:512]).astype(BF16)
        qvt_ref[:, rows] = mm_nt(wt_ref[...], n_ref[rows]).astype(BF16)
        return carry

    lax.fori_loop(0, 2, maps, 0)
    lane = lax.broadcasted_iota(jnp.int32, (1, 128), 1)
    low = lane < 64
    even = (lane // 32) % 2 == 0
    lowm = low.astype(BF16)
    highm = (lane >= 64).astype(BF16)
    groups = windows // 4

    def place(i, u):
        g = u % 2
        return g, slice(128 * g, 128 * g + 128), pl.multiple_of(256 * i + 128 * (u // 2), 128)

    def scores(i, u):
        g, cols, rows = place(i, u)
        qt = qvt_ref[cols, pl.ds(rows, 128)]
        turn = pltpu.roll(qt.astype(F32), 64, 1).astype(BF16)
        zero = jnp.zeros((32, 128), BF16)
        for side in range(2):
            straight = qt * (lowm if side == 0 else highm)
            rolled = turn * (highm if side == 0 else lowm)
            blocks = []
            for c in range(2):
                parts = [zero] * 4
                parts[2 * c] = straight[64 * c : 64 * c + 32]
                parts[2 * c + 1] = rolled[64 * c + 32 : 64 * c + 64]
                blocks.append(jnp.concatenate(parts, axis=0))
            keys = k_ref[pl.ds(rows + 64 * side, 64), cols]
            s_refs[u][64 * side : 64 * side + 64, :] = mm(keys, jnp.concatenate(blocks, axis=1))

    def soften(u):
        g = u % 2
        for side in range(2):
            rows = slice(64 * side, 64 * side + 64)
            for c in range(2):
                lanes = slice(128 * c, 128 * c + 128)
                s = s_refs[u][rows, lanes] * scale + bias_ref[g, rows, lanes]
                e = jnp.exp2(s - jnp.max(s, axis=0, keepdims=True))
                d_refs[u][side : side + 1, lanes] = 1.0 / jnp.sum(e, axis=0, keepdims=True)
                e_refs[u][rows, lanes] = e.astype(BF16)

    def mix(i, u):
        g, cols, rows = place(i, u)
        vt = qvt_ref[256 + 128 * g : 256 + 128 * g + 128, pl.ds(rows, 128)]
        r = mm(jnp.concatenate([vt * lowm, vt * highm], axis=0), e_refs[u][...])
        parts = []
        for j in range(4):
            lanes = slice(128 * (j // 2), 128 * (j // 2) + 128)
            a, b = r[32 * j : 32 * j + 32, lanes], r[128 + 32 * j : 128 + 32 * j + 32, lanes]
            da, db = d_refs[u][0:1, lanes], d_refs[u][1:2, lanes]
            if j % 2 == 1:
                a, b, da, db = b, a, db, da
            parts.append(jnp.where(low, a, b) * jnp.where(low, da, db))
        t = jnp.concatenate(parts, axis=0).T
        o = jnp.concatenate(
            [jnp.where(even, t[0:64], t[64:128]), jnp.where(even, t[64:128], t[0:64])], axis=0
        )
        o_ref[pl.ds(rows, 128), cols] = o.astype(BF16)

    def turn(i, stages):
        for step in range(6):
            if "mix" in stages and step < 4:
                mix(i - 1, step)
            if "soften" in stages and 1 <= step < 5:
                soften(step - 1)
            if "scores" in stages and step >= 2:
                scores(i + 1, step - 2)

    turn(-1, ("scores",))
    turn(0, ("soften", "scores"))

    def body(i, carry):
        turn(i, ("mix", "soften", "scores"))
        return carry

    lax.fori_loop(1, groups - 1, body, 0)
    turn(groups - 1, ("mix", "soften"))
    turn(groups, ("mix",))


def project_and_feed(x_ref, o_ref, g_ref, n_ref, out_w_ref, up_ref, down_ref, y_ref):
    block = x_ref.shape[0] // 2

    def half(i, carry):
        rows = pl.ds(pl.multiple_of(block * i, 256), block)
        y = x_ref[rows] + mm(o_ref[rows], out_w_ref[...])
        x_ref[rows] = y
        n_ref[rows] = norm(y)
        for p in range(4):
            lanes = slice(256 * p, 256 * p + 256)
            g_ref[:, lanes] = gelu2(mm(n_ref[rows], up_ref[:, lanes])).astype(BF16)
        y_ref[rows] = x_ref[rows] + 0.5 * mm(g_ref[...], down_ref[...])
        return carry

    lax.fori_loop(0, 2, half, 0)


def local_kernel(
    first, strips,
    x_ref, above_ref, below_ref, left_ref, right_ref,
    ew_ref, dw_ref, pw_ref, qkv_ref, wt_ref, table_ref, index_ref, out_w_ref, up_ref, down_ref,
    res_ref,
    hid0_ref, hid1_ref, act0_ref, act1_ref, xn_ref,
    bias_ref, xw_ref, n_ref, k_ref, qvt_ref, o_ref, g_ref, y_ref, *units
):
    rows = 8 * strips
    last = x_ref.shape[0]
    hids, acts = (hid0_ref, hid1_ref), (act0_ref, act1_ref)
    make_bias(table_ref, index_ref, bias_ref)

    for r in range(2):
        image = 8 * first + r - 1
        x = above_ref[0] if image < 0 else x_ref[image]
        xn_ref[64 * r : 64 * r + 64] = norm(x.astype(F32))
    for i, ref in enumerate((left_ref, right_ref)):
        xn_ref[128 + 64 * i : 128 + 64 * i + rows + 2] = norm(
            ref[8 * first : 8 * first + rows + 2].astype(F32)
        )

    def normalize(strip, carry):
        x = x_ref[pl.ds(8 * (first + strip) + 1, 8)].reshape(512, 256)
        xn_ref[pl.ds(pl.multiple_of(512 * strip + 256, 256), 512)] = norm(x.astype(F32))
        return carry

    ends = 8 * (first + strips) >= last
    lax.fori_loop(0, strips - 1 if ends else strips, normalize, 0)
    if ends:
        at = 512 * (strips - 1) + 256
        x = x_ref[last - 7 : last].reshape(448, 256)
        xn_ref[at : at + 448] = norm(x.astype(F32))
        xn_ref[at + 448 : at + 512] = norm(below_ref[0].astype(F32))

    def hidden_border(p, hid):
        h = gelu2(mm(xn_ref[0:256], ew_ref[:, 256 * p : 256 * p + 256])).astype(F32)
        for c in range(2):
            lanes = slice(128 * c, 128 * c + 128)
            hid[c, 0:2, 8:72, :] = h[0:128, lanes].reshape(2, 64, 128)
            for r in range(rows + 2):
                hid[c, r, 7:8, :] = h[128 + r : 129 + r, lanes]
                hid[c, r, 72:73, :] = h[192 + r : 193 + r, lanes]

    def hidden_part(p, hid, strip, part):
        at = pl.multiple_of(512 * strip + 256 + 256 * part, 256)
        h = gelu2(mm(xn_ref[pl.ds(at, 256)], ew_ref[:, 256 * p : 256 * p + 256])).astype(F32)
        for c in range(2):
            lanes = slice(128 * c, 128 * c + 128)
            hid[c, pl.ds(8 * strip + 2 + 4 * part, 4), 8:72, :] = h[:, lanes].reshape(4, 64, 128)

    def project_part(p, act, strip, part):
        at = pl.ds(pl.multiple_of(512 * strip + 256 * part, 256), 256)
        d = mm(act[at], pw_ref[256 * p : 256 * p + 256, :])
        y_ref[at] = d if p == 0 else y_ref[at] + d

    def conv_part(p, hid, act, strip, c, half):
        w = (dw_ref[:, 256 * p + 128 * c : 256 * p + 128 * c + 128] * 0.5).astype(BF16)
        begin = 7 + 32 * half
        acc = [None] * 8
        for ir in range(10):
            h = [hid[c, 8 * strip + ir, begin + d : begin + d + 32, :].astype(BF16) for d in range(3)]
            for dy in range(3):
                orow = ir - dy
                if 0 <= orow < 8:
                    t = h[0] * w[3 * dy : 3 * dy + 1] + h[1] * w[3 * dy + 1 : 3 * dy + 2]
                    t = t + h[2] * w[3 * dy + 2 : 3 * dy + 3]
                    acc[orow] = t if acc[orow] is None else acc[orow] + t
            if ir >= 2:
                to = pl.multiple_of(512 * strip + 64 * (ir - 2) + 32 * half, 32)
                act[pl.ds(to, 32), 128 * c : 128 * c + 128] = gelu2(acc[ir - 2])

    def first_hidden(strip, carry):
        for part in range(2):
            hidden_part(0, hids[0], strip, part)
        return carry

    hidden_border(0, hids[0])
    lax.fori_loop(0, strips, first_hidden, 0)
    for p in range(4):
        if p < 3:
            hidden_border(p + 1, hids[(p + 1) % 2])

        def quarter(strip, carry, p=p):
            for c in range(2):
                for half in range(2):
                    if half == 0 and p < 3:
                        hidden_part(p + 1, hids[(p + 1) % 2], strip, c)
                    if half == 1 and p > 0:
                        project_part(p - 1, acts[(p - 1) % 2], strip, c)
                    conv_part(p, hids[p % 2], acts[p % 2], strip, c, half)
            return carry

        lax.fori_loop(0, strips, quarter, 0)

    def gather(strip, carry):
        at = pl.ds(pl.multiple_of(512 * strip, 512), 512)
        x = x_ref[pl.ds(8 * (first + strip), 8)].reshape(512, 256).astype(F32)
        y = y_ref[at] + mm(acts[1][at], pw_ref[768:1024, :])
        y = (x + 0.5 * y).reshape(8, 64, 256)
        for w in range(8):
            to = pl.ds(pl.multiple_of(512 * strip + 64 * w, 64), 64)
            x = y[:, 8 * w : 8 * w + 8].reshape(64, 256)
            xw_ref[to] = x
            n_ref[to] = norm(x)
        return carry

    lax.fori_loop(0, strips, gather, 0)
    attend(8 * strips, n_ref, qkv_ref, wt_ref, bias_ref, k_ref, qvt_ref, o_ref, units[0:4], units[4:8], units[8:12])
    project_and_feed(xw_ref, o_ref, g_ref, n_ref, out_w_ref, up_ref, down_ref, y_ref)

    def spread(strip, carry):
        for w in range(8):
            y = y_ref[pl.ds(pl.multiple_of(512 * strip + 64 * w, 64), 64)]
            res_ref[pl.ds(8 * strip, 8), 8 * w : 8 * w + 8, :] = y.reshape(8, 8, 256).astype(BF16)
        return carry

    lax.fori_loop(0, strips, spread, 0)


def grid_kernel(
    windows,
    x_ref, qkv_ref, wt_ref, table_ref, index_ref, out_w_ref, up_ref, down_ref,
    res_ref,
    xs_ref, bias_ref, xw_ref, n_ref, k_ref, qvt_ref, o_ref, g_ref, y_ref, *units
):
    make_bias(table_ref, index_ref, bias_ref)
    x = x_ref[...].astype(F32).reshape(64 * windows, 256)
    xs_ref[0] = x[:, 0:128]
    xs_ref[1] = x[:, 128:256]
    for w in range(windows):
        rows = slice(64 * w, 64 * w + 64)
        for half in range(2):
            xw_ref[rows, 128 * half : 128 * half + 128] = xs_ref[half, pl.ds(w, 64, stride=windows), :]
    n_ref[...] = norm(xw_ref[...])
    attend(windows, n_ref, qkv_ref, wt_ref, bias_ref, k_ref, qvt_ref, o_ref, units[0:4], units[4:8], units[8:12])
    project_and_feed(xw_ref, o_ref, g_ref, n_ref, out_w_ref, up_ref, down_ref, y_ref)
    for w in range(windows):
        rows = slice(64 * w, 64 * w + 64)
        for half in range(2):
            xs_ref[half, pl.ds(w, 64, stride=windows), :] = y_ref[rows, 128 * half : 128 * half + 128]
    y = jnp.concatenate([xs_ref[0], xs_ref[1]], axis=1)
    res_ref[...] = y.reshape(64, windows, 256).astype(BF16)


def attend_scratch(windows):
    rows = 64 * windows
    return [
        pltpu.VMEM((2, 128, 256), F32),
        pltpu.VMEM((rows, 256), F32),
        pltpu.VMEM((rows, 256), BF16),
        pltpu.VMEM((rows, 256), BF16),
        pltpu.VMEM((512, rows), BF16),
        pltpu.VMEM((rows, 256), BF16),
        pltpu.VMEM((rows // 2, 1024), BF16),
        pltpu.VMEM((rows, 256), F32),
    ] + [pltpu.VMEM((128, 256), F32)] * 4 + [pltpu.VMEM((128, 256), BF16)] * 4 + [pltpu.VMEM((2, 256), F32)] * 4


def in_vmem(count):
    return [pl.BlockSpec(memory_space=pltpu.VMEM)] * count


def local_stage(first, strips, cells, weights):
    ops = tuple(cells) + tuple(weights)
    rows = 8 * strips
    return pl.pallas_call(
        functools.partial(local_kernel, first, strips),
        in_specs=in_vmem(len(ops)),
        out_specs=in_vmem(1)[0],
        out_shape=jax.ShapeDtypeStruct((rows, 64, 256), BF16),
        scratch_shapes=[
            pltpu.VMEM((2, rows + 2, WIDE, 128), F32),
            pltpu.VMEM((2, rows + 2, WIDE, 128), F32),
            pltpu.VMEM((64 * rows, 256), BF16),
            pltpu.VMEM((64 * rows, 256), BF16),
            pltpu.VMEM((64 * rows + 256, 256), BF16),
        ]
        + attend_scratch(8 * strips),
        compiler_params=PARAMS,
        name="local_stage",
    )(*ops)


def grid_stage(x, weights):
    windows = x.shape[1]
    ops = (x,) + tuple(weights)
    return pl.pallas_call(
        functools.partial(grid_kernel, windows),
        in_specs=in_vmem(len(ops)),
        out_specs=in_vmem(1)[0],
        out_shape=jax.ShapeDtypeStruct(x.shape, BF16),
        scratch_shapes=[pltpu.VMEM((2, 64 * windows, 128), F32)] + attend_scratch(windows),
        compiler_params=PARAMS,
        name="grid_stage",
    )(*ops)


def bias_operands(table, index):
    turned_index = index.T
    return (
        jnp.pad(table.T, ((0, 0), (0, 256 - table.shape[0]))),
        jnp.concatenate([turned_index, turned_index], axis=1),
    )


def turned(qkv):
    return jnp.concatenate([qkv[:, :256], qkv[:, 512:]], axis=1).T


def neighbours(before, after, axes):
    count = lax.axis_size(axes)
    up = [(i, i + 1) for i in range(count - 1)]
    down = [(j, i) for i, j in up]
    return lax.ppermute(before, axes, up), lax.ppermute(after, axes, down)


def on_device(
    field, expand_w, dw_kernel, project_w,
    blk_qkv, blk_out, blk_table, blk_index, blk_up, blk_down,
    grid_qkv, grid_out, grid_table, grid_index, grid_up, grid_down,
):
    rows, cols, width = field.shape
    above, below = neighbours(field[-1:], field[:1], "ha")
    first = jnp.concatenate([above[:, 0], field[:, 0], below[:, 0]], axis=0)
    final = jnp.concatenate([above[:, -1], field[:, -1], below[:, -1]], axis=0)
    left, right = neighbours(final, first, ("wh", "core"))
    cells = (field, above, below, left, right)
    local_w = (expand_w, dw_kernel, project_w, blk_qkv, turned(blk_qkv))
    local_w += bias_operands(blk_table, blk_index) + (blk_out, blk_up, blk_down)
    grid_w = (grid_qkv, turned(grid_qkv)) + bias_operands(grid_table, grid_index)
    grid_w += (grid_out, grid_up, grid_down)
    outs = []
    start = 0
    for strips in CHUNKS:
        part = local_stage(start, strips, cells, local_w)
        start += strips
        part = part.reshape(64, strips * 8, width)
        moved = lax.all_to_all(part, ("ha", "wh"), 0, 0, tiled=True)
        done = grid_stage(moved, grid_w)
        back = lax.all_to_all(done, ("ha", "wh"), 0, 0, tiled=True)
        outs.append(back.reshape(strips * 8, cols, width))
    return outs[0] if len(outs) == 1 else jnp.concatenate(outs, axis=0)


def solution(mesh):
    split = Mesh(mesh.devices.reshape(8, 8, 2), ("ha", "wh", "core"))
    spec = P("ha", ("wh", "core"), None)
    return jax.shard_map(
        on_device, mesh=split, in_specs=(spec,) + (P(),) * 15, out_specs=spec, check_vma=False
    )
```

```python
import functools
import math

import jax
import jax.numpy as jnp
from jax import lax
from jax.experimental import pallas as pl
from jax.experimental.pallas import tpu as pltpu
from jax.sharding import Mesh
from jax.sharding import PartitionSpec as P

EPS = 1e-05
LOG2E = 1.4426950408889634
C0 = 0.7978845608028654
C1 = C0 * 0.044715
F32 = jnp.float32
BF16 = jnp.bfloat16
WIDE = 80
UNITS = 8
CHUNKS = (6,)
PARAMS = pltpu.CompilerParams(vmem_limit_bytes=56 << 20)


def norm(x):
    center = x - jnp.sum(x, axis=-1, keepdims=True) * (1.0 / 256.0)
    spread = jnp.sum(center * center, axis=-1, keepdims=True) * (1.0 / 256.0)
    return (center * lax.rsqrt(spread + EPS)).astype(BF16)


def gelu2(v):
    v = v.astype(BF16)
    u = v * (jnp.asarray(C1, BF16) * (v * v) + jnp.asarray(C0, BF16))
    return v + v * jnp.tanh(u)


def mm(a, b):
    return jnp.dot(a, b, preferred_element_type=F32)


def mm_nt(a, b):
    return lax.dot_general(a, b, (((1,), (1,)), ((), ())), preferred_element_type=F32)


def fetch(sources, targets, sems):
    copies = [
        pltpu.make_async_copy(source, target, sems.at[i])
        for i, (source, target) in enumerate(zip(sources, targets))
    ]
    for copy in copies:
        copy.start()
    return copies


def make_bias(table_ref, index_ref, bias_ref):
    index = index_ref[...]
    low = lax.broadcasted_iota(jnp.int32, (64, 128), 1) < 64
    upper = index >= 128
    within = jnp.bitwise_and(index, 127)
    got = []
    for h in range(8):
        halves = []
        for half in range(2):
            row = jnp.broadcast_to(table_ref[h : h + 1, 128 * half : 128 * half + 128] * LOG2E, (64, 128))
            halves.append(jnp.take_along_axis(row, within, axis=1))
        got.append(jnp.where(upper, halves[1], halves[0]))
    for h in range(0, 8, 2):
        g, c = h // 4, (h % 4) // 2
        lanes = slice(128 * c, 128 * c + 128)
        bias_ref[g, 0:64, lanes] = jnp.where(low, got[h], got[h + 1])
        bias_ref[g, 64:128, lanes] = jnp.where(low, got[h + 1], got[h])


def attend(windows, n_ref, qkv_ref, wt_ref, bias_ref, k_ref, qvt_ref, o_ref, s_refs, e_refs, d_refs):
    scale = LOG2E / math.sqrt(32.0)
    block = 64 * windows // 2

    def maps(i, carry):
        rows = pl.ds(pl.multiple_of(block * i, 256), block)
        k_ref[rows] = mm(n_ref[rows], qkv_ref[:, 256:512]).astype(BF16)
        qvt_ref[:, rows] = mm_nt(wt_ref[...], n_ref[rows]).astype(BF16)
        return carry

    lax.fori_loop(0, 2, maps, 0)
    lane = lax.broadcasted_iota(jnp.int32, (1, 128), 1)
    low = lane < 64
    even = (lane // 32) % 2 == 0
    lowm = low.astype(BF16)
    highm = (lane >= 64).astype(BF16)
    groups = windows // UNITS

    def place(i, u):
        g = u % 2
        return g, slice(128 * g, 128 * g + 128), pl.multiple_of(64 * UNITS * i + 128 * (u // 2), 128)

    def scores(i, u):
        g, cols, rows = place(i, u)
        qt = qvt_ref[cols, pl.ds(rows, 128)]
        turn = pltpu.roll(qt.astype(F32), 64, 1).astype(BF16)
        zero = jnp.zeros((32, 128), BF16)
        for side in range(2):
            straight = qt * (lowm if side == 0 else highm)
            rolled = turn * (highm if side == 0 else lowm)
            blocks = []
            for c in range(2):
                parts = [zero] * 4
                parts[2 * c] = straight[64 * c : 64 * c + 32]
                parts[2 * c + 1] = rolled[64 * c + 32 : 64 * c + 64]
                blocks.append(jnp.concatenate(parts, axis=0))
            keys = k_ref[pl.ds(rows + 64 * side, 64), cols]
            s_refs[u][64 * side : 64 * side + 64, :] = mm(keys, jnp.concatenate(blocks, axis=1))

    def soften(u):
        g = u % 2
        for side in range(2):
            rows = slice(64 * side, 64 * side + 64)
            for c in range(2):
                lanes = slice(128 * c, 128 * c + 128)
                s = s_refs[u][rows, lanes] * scale + bias_ref[g, rows, lanes]
                e = jnp.exp2(s - jnp.max(s, axis=0, keepdims=True))
                d_refs[u][side : side + 1, lanes] = 1.0 / jnp.sum(e, axis=0, keepdims=True)
                e_refs[u][rows, lanes] = e.astype(BF16)

    def mix(i, u):
        g, cols, rows = place(i, u)
        vt = qvt_ref[256 + 128 * g : 256 + 128 * g + 128, pl.ds(rows, 128)]
        r = mm(jnp.concatenate([vt * lowm, vt * highm], axis=0), e_refs[u][...])
        parts = []
        for j in range(4):
            lanes = slice(128 * (j // 2), 128 * (j // 2) + 128)
            a, b = r[32 * j : 32 * j + 32, lanes], r[128 + 32 * j : 128 + 32 * j + 32, lanes]
            da, db = d_refs[u][0:1, lanes], d_refs[u][1:2, lanes]
            if j % 2 == 1:
                a, b, da, db = b, a, db, da
            parts.append(jnp.where(low, a, b) * jnp.where(low, da, db))
        t = jnp.concatenate(parts, axis=0).T
        o = jnp.concatenate(
            [jnp.where(even, t[0:64], t[64:128]), jnp.where(even, t[64:128], t[0:64])], axis=0
        )
        o_ref[pl.ds(rows, 128), cols] = o.astype(BF16)

    def turn(i, stages):
        for step in range(UNITS + 2):
            if "mix" in stages and step < UNITS:
                mix(i - 1, step)
            if "soften" in stages and 1 <= step < UNITS + 1:
                soften(step - 1)
            if "scores" in stages and step >= 2:
                scores(i + 1, step - 2)

    turn(-1, ("scores",))
    turn(0, ("soften", "scores"))

    def body(i, carry):
        turn(i, ("mix", "soften", "scores"))
        return carry

    lax.fori_loop(1, groups - 1, body, 0)
    turn(groups - 1, ("mix", "soften"))
    turn(groups, ("mix",))


def project_and_feed(x_ref, o_ref, g_ref, n_ref, out_w_ref, up_ref, down_ref, y_ref):
    block = x_ref.shape[0] // 2

    def half(i, carry):
        rows = pl.ds(pl.multiple_of(block * i, 256), block)
        y = x_ref[rows] + mm(o_ref[rows], out_w_ref[...])
        x_ref[rows] = y
        n_ref[rows] = norm(y)
        for p in range(4):
            lanes = slice(256 * p, 256 * p + 256)
            g_ref[:, lanes] = gelu2(mm(n_ref[rows], up_ref[:, lanes])).astype(BF16)
        y_ref[rows] = x_ref[rows] + 0.5 * mm(g_ref[...], down_ref[...])
        return carry

    lax.fori_loop(0, 2, half, 0)


def local_kernel(
    first, strips,
    x_ref, above_ref, below_ref, left_ref, right_ref,
    ew_ref, dw_ref, table_ref, index_ref, *rest
):
    late, rest = rest[:6], rest[6:]
    res_ref, hid_ref, act_ref, xn_ref, sems = rest[:5]
    pw_ref, qkv_ref, wt_ref, out_w_ref, up_ref, down_ref = rest[5:11]
    bias_ref, xw_ref, n_ref, k_ref, qvt_ref, o_ref, g_ref, y_ref = rest[11:19]
    units = rest[19:]
    copies = fetch(late, rest[5:11], sems)
    rows = 8 * strips
    last = x_ref.shape[0]
    make_bias(table_ref, index_ref, bias_ref)

    for r in range(2):
        image = 8 * first + r - 1
        x = above_ref[0] if image < 0 else x_ref[image]
        xn_ref[64 * r : 64 * r + 64] = norm(x.astype(F32))
    for i, ref in enumerate((left_ref, right_ref)):
        xn_ref[128 + 64 * i : 128 + 64 * i + rows + 2] = norm(
            ref[8 * first : 8 * first + rows + 2].astype(F32)
        )

    def normalize(strip, carry):
        x = x_ref[pl.ds(8 * (first + strip) + 1, 8)].reshape(512, 256)
        xn_ref[pl.ds(pl.multiple_of(512 * strip + 256, 256), 512)] = norm(x.astype(F32))
        return carry

    ends = 8 * (first + strips) >= last
    lax.fori_loop(0, strips - 1 if ends else strips, normalize, 0)
    if ends:
        at = 512 * (strips - 1) + 256
        x = x_ref[last - 7 : last].reshape(448, 256)
        xn_ref[at : at + 448] = norm(x.astype(F32))
        xn_ref[at + 448 : at + 512] = norm(below_ref[0].astype(F32))

    def hidden_border(p):
        h = gelu2(mm(xn_ref[0:256], ew_ref[:, 256 * p : 256 * p + 256])).astype(F32)
        for c in range(2):
            lanes = slice(128 * c, 128 * c + 128)
            hid_ref[c, 0:2, 8:72, :] = h[0:128, lanes].reshape(2, 64, 128)
            for r in range(rows + 2):
                hid_ref[c, r, 7:8, :] = h[128 + r : 129 + r, lanes]
                hid_ref[c, r, 72:73, :] = h[192 + r : 193 + r, lanes]

    def hidden_part(p, part):
        at = pl.multiple_of(256 * strips * part + 256, 256)
        h = gelu2(mm(xn_ref[pl.ds(at, 256 * strips)], ew_ref[:, 256 * p : 256 * p + 256])).astype(F32)
        for c in range(2):
            lanes = slice(128 * c, 128 * c + 128)
            hid_ref[c, pl.ds(4 * strips * part + 2, 4 * strips), 8:72, :] = h[:, lanes].reshape(
                4 * strips, 64, 128
            )

    def conv_part(p, strip, c, half):
        w = (dw_ref[:, 256 * p + 128 * c : 256 * p + 128 * c + 128] * 0.5).astype(BF16)
        begin = 7 + 32 * half
        acc = [None] * 8
        for ir in range(10):
            h = [hid_ref[c, 8 * strip + ir, begin + d : begin + d + 32, :].astype(BF16) for d in range(3)]
            for dy in range(3):
                orow = ir - dy
                if 0 <= orow < 8:
                    t = h[0] * w[3 * dy : 3 * dy + 1] + h[1] * w[3 * dy + 1 : 3 * dy + 2]
                    t = t + h[2] * w[3 * dy + 2 : 3 * dy + 3]
                    acc[orow] = t if acc[orow] is None else acc[orow] + t
            if ir >= 2:
                to = pl.multiple_of(512 * strip + 64 * (ir - 2) + 32 * half, 32)
                lanes = slice(256 * p + 128 * c, 256 * p + 128 * c + 128)
                act_ref[pl.ds(to, 32), lanes] = gelu2(acc[ir - 2])

    for p in range(4):
        hidden_border(p)

        def hidden(part, carry, p=p):
            hidden_part(p, part)
            return carry

        def conv(strip, carry, p=p):
            for c in range(2):
                for half in range(2):
                    conv_part(p, strip, c, half)
            return carry

        lax.fori_loop(0, 2, hidden, 0)
        lax.fori_loop(0, strips, conv, 0)

    def project(part, carry):
        at = pl.ds(pl.multiple_of(256 * strips * part, 256), 256 * strips)
        y_ref[at] = mm(act_ref[at], pw_ref[...])
        return carry

    def gather(strip, carry):
        at = pl.ds(pl.multiple_of(512 * strip, 512), 512)
        x = x_ref[pl.ds(8 * (first + strip), 8)].reshape(512, 256).astype(F32)
        y = (x + 0.5 * y_ref[at]).reshape(8, 64, 256)
        for w in range(8):
            to = pl.ds(pl.multiple_of(512 * strip + 64 * w, 64), 64)
            x = y[:, 8 * w : 8 * w + 8].reshape(64, 256)
            xw_ref[to] = x
            n_ref[to] = norm(x)
        return carry

    copies[0].wait()
    lax.fori_loop(0, 2, project, 0)
    lax.fori_loop(0, strips, gather, 0)
    for copy in copies[1:3]:
        copy.wait()
    attend(8 * strips, n_ref, qkv_ref, wt_ref, bias_ref, k_ref, qvt_ref, o_ref, units[:UNITS], units[UNITS : 2 * UNITS], units[2 * UNITS :])
    for copy in copies[3:]:
        copy.wait()
    project_and_feed(xw_ref, o_ref, g_ref, n_ref, out_w_ref, up_ref, down_ref, y_ref)

    def spread(strip, carry):
        for w in range(8):
            y = y_ref[pl.ds(pl.multiple_of(512 * strip + 64 * w, 64), 64)]
            res_ref[pl.ds(8 * strip, 8), 8 * w : 8 * w + 8, :] = y.reshape(8, 8, 256).astype(BF16)
        return carry

    lax.fori_loop(0, strips, spread, 0)


def grid_kernel(
    windows,
    x_ref, qkv_ref, wt_ref, table_ref, index_ref, late0_ref, late1_ref, late2_ref,
    res_ref,
    xs_ref, sems, out_w_ref, up_ref, down_ref, bias_ref, xw_ref, n_ref, k_ref, qvt_ref, o_ref, g_ref, y_ref, *units
):
    copies = fetch((late0_ref, late1_ref, late2_ref), (out_w_ref, up_ref, down_ref), sems)
    make_bias(table_ref, index_ref, bias_ref)
    x = x_ref[...].astype(F32).reshape(64 * windows, 256)
    xs_ref[0] = x[:, 0:128]
    xs_ref[1] = x[:, 128:256]
    for w in range(windows):
        rows = slice(64 * w, 64 * w + 64)
        for half in range(2):
            xw_ref[rows, 128 * half : 128 * half + 128] = xs_ref[half, pl.ds(w, 64, stride=windows), :]
    n_ref[...] = norm(xw_ref[...])
    attend(windows, n_ref, qkv_ref, wt_ref, bias_ref, k_ref, qvt_ref, o_ref, units[:UNITS], units[UNITS : 2 * UNITS], units[2 * UNITS :])
    for copy in copies:
        copy.wait()
    project_and_feed(xw_ref, o_ref, g_ref, n_ref, out_w_ref, up_ref, down_ref, y_ref)
    for w in range(windows):
        rows = slice(64 * w, 64 * w + 64)
        for half in range(2):
            xs_ref[half, pl.ds(w, 64, stride=windows), :] = y_ref[rows, 128 * half : 128 * half + 128]
    y = jnp.concatenate([xs_ref[0], xs_ref[1]], axis=1)
    res_ref[...] = y.reshape(64, windows, 256).astype(BF16)


UNIT_SCRATCH = (((128, 256), F32), ((128, 256), BF16), ((2, 256), F32))


def attend_scratch(windows):
    rows = 64 * windows
    return [
        pltpu.VMEM((2, 128, 256), F32),
        pltpu.VMEM((rows, 256), F32),
        pltpu.VMEM((rows, 256), BF16),
        pltpu.VMEM((rows, 256), BF16),
        pltpu.VMEM((512, rows), BF16),
        pltpu.VMEM((rows, 256), BF16),
        pltpu.VMEM((rows // 2, 1024), BF16),
        pltpu.VMEM((rows, 256), F32),
    ] + [pltpu.VMEM(shape, kind) for shape, kind in UNIT_SCRATCH for _ in range(UNITS)]


def landing(arrays):
    return [pltpu.SemaphoreType.DMA((len(arrays),))] + [pltpu.VMEM(a.shape, a.dtype) for a in arrays]


def in_hbm(count):
    return [pl.BlockSpec(memory_space=pl.ANY)] * count


def in_vmem(count):
    return [pl.BlockSpec(memory_space=pltpu.VMEM)] * count


def local_stage(first, strips, cells, early, late):
    ops = tuple(cells) + tuple(early) + tuple(late)
    rows = 8 * strips
    return pl.pallas_call(
        functools.partial(local_kernel, first, strips),
        in_specs=in_vmem(len(cells) + len(early)) + in_hbm(len(late)),
        out_specs=in_vmem(1)[0],
        out_shape=jax.ShapeDtypeStruct((rows, 64, 256), BF16),
        scratch_shapes=[
            pltpu.VMEM((2, rows + 2, WIDE, 128), F32),
            pltpu.VMEM((64 * rows, 1024), BF16),
            pltpu.VMEM((64 * rows + 256, 256), BF16),
        ]
        + landing(late)
        + attend_scratch(8 * strips),
        compiler_params=PARAMS,
        name="local_stage",
    )(*ops)


def grid_stage(x, early, late):
    windows = x.shape[1]
    ops = (x,) + tuple(early) + tuple(late)
    return pl.pallas_call(
        functools.partial(grid_kernel, windows),
        in_specs=in_vmem(1 + len(early)) + in_hbm(len(late)),
        out_specs=in_vmem(1)[0],
        out_shape=jax.ShapeDtypeStruct(x.shape, BF16),
        scratch_shapes=[pltpu.VMEM((2, 64 * windows, 128), F32)] + landing(late) + attend_scratch(windows),
        compiler_params=PARAMS,
        name="grid_stage",
    )(*ops)


def bias_operands(table, index):
    turned_index = index.T
    return (
        jnp.pad(table.T, ((0, 0), (0, 256 - table.shape[0]))),
        jnp.concatenate([turned_index, turned_index], axis=1),
    )


def turned(qkv):
    return jnp.concatenate([qkv[:, :256], qkv[:, 512:]], axis=1).T


def neighbours(before, after, axes):
    count = lax.axis_size(axes)
    up = [(i, i + 1) for i in range(count - 1)]
    down = [(j, i) for i, j in up]
    return lax.ppermute(before, axes, up), lax.ppermute(after, axes, down)


def on_device(
    field, expand_w, dw_kernel, project_w,
    blk_qkv, blk_out, blk_table, blk_index, blk_up, blk_down,
    grid_qkv, grid_out, grid_table, grid_index, grid_up, grid_down,
):
    rows, cols, width = field.shape
    above, below = neighbours(field[-1:], field[:1], "ha")
    first = jnp.concatenate([above[:, 0], field[:, 0], below[:, 0]], axis=0)
    final = jnp.concatenate([above[:, -1], field[:, -1], below[:, -1]], axis=0)
    left, right = neighbours(final, first, ("wh", "core"))
    cells = (field, above, below, left, right)
    local_w = (expand_w, dw_kernel) + bias_operands(blk_table, blk_index)
    local_late = (project_w, blk_qkv, turned(blk_qkv), blk_out, blk_up, blk_down)
    grid_w = (grid_qkv, turned(grid_qkv)) + bias_operands(grid_table, grid_index)
    grid_late = (grid_out, grid_up, grid_down)
    outs = []
    start = 0
    for strips in CHUNKS:
        part = local_stage(start, strips, cells, local_w, local_late)
        start += strips
        part = part.reshape(64, strips * 8, width)
        moved = lax.all_to_all(part, ("ha", "wh"), 0, 0, tiled=True)
        done = grid_stage(moved, grid_w, grid_late)
        back = lax.all_to_all(done, ("ha", "wh"), 0, 0, tiled=True)
        outs.append(back.reshape(strips * 8, cols, width))
    return outs[0] if len(outs) == 1 else jnp.concatenate(outs, axis=0)


def solution(mesh):
    split = Mesh(mesh.devices.reshape(8, 8, 2), ("ha", "wh", "core"))
    spec = P("ha", ("wh", "core"), None)
    return jax.shard_map(
        on_device, mesh=split, in_specs=(spec,) + (P(),) * 15, out_specs=spec, check_vma=False
    )
```

```python
import functools
import math

import jax
import jax.numpy as jnp
from jax import lax
from jax.experimental import pallas as pl
from jax.experimental.pallas import tpu as pltpu
from jax.sharding import Mesh
from jax.sharding import PartitionSpec as P

EPS = 1e-05
LOG2E = 1.4426950408889634
C0 = 0.7978845608028654
C1 = C0 * 0.044715
F32 = jnp.float32
BF16 = jnp.bfloat16
WIDE = 80
UNITS = 8
CHUNKS = (6,)
PARAMS = pltpu.CompilerParams(vmem_limit_bytes=56 << 20)


def norm(x):
    center = x - jnp.sum(x, axis=-1, keepdims=True) * (1.0 / 256.0)
    spread = jnp.sum(center * center, axis=-1, keepdims=True) * (1.0 / 256.0)
    return (center * lax.rsqrt(spread + EPS)).astype(BF16)


def gelu2(v):
    v = v.astype(BF16)
    u = v * (jnp.asarray(C1, BF16) * (v * v) + jnp.asarray(C0, BF16))
    return v + v * jnp.tanh(u)


def mm(a, b):
    return jnp.dot(a, b, preferred_element_type=F32)


def mm_nt(a, b):
    return lax.dot_general(a, b, (((1,), (1,)), ((), ())), preferred_element_type=F32)


def fetch(sources, targets, sems):
    copies = [
        pltpu.make_async_copy(source, target, sems.at[i])
        for i, (source, target) in enumerate(zip(sources, targets))
    ]
    for copy in copies:
        copy.start()
    return copies


def make_bias(table_ref, index_ref, bias_ref):
    index = index_ref[...]
    low = lax.broadcasted_iota(jnp.int32, (64, 128), 1) < 64
    upper = index >= 128
    within = jnp.bitwise_and(index, 127)
    got = []
    for h in range(8):
        halves = []
        for half in range(2):
            row = jnp.broadcast_to(table_ref[h : h + 1, 128 * half : 128 * half + 128] * LOG2E, (64, 128))
            halves.append(jnp.take_along_axis(row, within, axis=1))
        got.append(jnp.where(upper, halves[1], halves[0]))
    for h in range(0, 8, 2):
        g, c = h // 4, (h % 4) // 2
        lanes = slice(128 * c, 128 * c + 128)
        bias_ref[g, 0:64, lanes] = jnp.where(low, got[h], got[h + 1])
        bias_ref[g, 64:128, lanes] = jnp.where(low, got[h + 1], got[h])


def attend(windows, n_ref, qkv_ref, wt_ref, bias_ref, k_ref, qvt_ref, o_ref, s_refs, e_refs, d_refs):
    scale = LOG2E / math.sqrt(32.0)
    block = 64 * windows // 2

    def maps(i, carry):
        rows = pl.ds(pl.multiple_of(block * i, 256), block)
        k_ref[rows] = mm(n_ref[rows], qkv_ref[:, 256:512]).astype(BF16)
        qvt_ref[:, rows] = mm_nt(wt_ref[...], n_ref[rows]).astype(BF16)
        return carry

    lax.fori_loop(0, 2, maps, 0)
    lane = lax.broadcasted_iota(jnp.int32, (1, 128), 1)
    low = lane < 64
    even = (lane // 32) % 2 == 0
    lowm = low.astype(BF16)
    highm = (lane >= 64).astype(BF16)
    groups = windows // UNITS

    def place(i, u):
        g = u % 2
        return g, slice(128 * g, 128 * g + 128), pl.multiple_of(64 * UNITS * i + 128 * (u // 2), 128)

    def scores(i, u):
        g, cols, rows = place(i, u)
        qt = qvt_ref[cols, pl.ds(rows, 128)]
        turn = pltpu.roll(qt.astype(F32), 64, 1).astype(BF16)
        zero = jnp.zeros((32, 128), BF16)
        for side in range(2):
            straight = qt * (lowm if side == 0 else highm)
            rolled = turn * (highm if side == 0 else lowm)
            blocks = []
            for c in range(2):
                parts = [zero] * 4
                parts[2 * c] = straight[64 * c : 64 * c + 32]
                parts[2 * c + 1] = rolled[64 * c + 32 : 64 * c + 64]
                blocks.append(jnp.concatenate(parts, axis=0))
            keys = k_ref[pl.ds(rows + 64 * side, 64), cols]
            s_refs[u][64 * side : 64 * side + 64, :] = mm(keys, jnp.concatenate(blocks, axis=1))

    def soften(u):
        g = u % 2
        for side in range(2):
            rows = slice(64 * side, 64 * side + 64)
            for c in range(2):
                lanes = slice(128 * c, 128 * c + 128)
                s = s_refs[u][rows, lanes] * scale + bias_ref[g, rows, lanes]
                e = jnp.exp2(s - jnp.max(s, axis=0, keepdims=True))
                d_refs[u][side : side + 1, lanes] = 1.0 / jnp.sum(e, axis=0, keepdims=True)
                e_refs[u][rows, lanes] = e.astype(BF16)

    def mix(i, u):
        g, cols, rows = place(i, u)
        vt = qvt_ref[256 + 128 * g : 256 + 128 * g + 128, pl.ds(rows, 128)]
        r = mm(jnp.concatenate([vt * lowm, vt * highm], axis=0), e_refs[u][...])
        parts = []
        for j in range(4):
            lanes = slice(128 * (j // 2), 128 * (j // 2) + 128)
            a, b = r[32 * j : 32 * j + 32, lanes], r[128 + 32 * j : 128 + 32 * j + 32, lanes]
            da, db = d_refs[u][0:1, lanes], d_refs[u][1:2, lanes]
            if j % 2 == 1:
                a, b, da, db = b, a, db, da
            parts.append(jnp.where(low, a, b) * jnp.where(low, da, db))
        t = jnp.concatenate(parts, axis=0).T
        o = jnp.concatenate(
            [jnp.where(even, t[0:64], t[64:128]), jnp.where(even, t[64:128], t[0:64])], axis=0
        )
        o_ref[pl.ds(rows, 128), cols] = o.astype(BF16)

    def turn(i, stages):
        for step in range(UNITS + 2):
            if "mix" in stages and step < UNITS:
                mix(i - 1, step)
            if "soften" in stages and 1 <= step < UNITS + 1:
                soften(step - 1)
            if "scores" in stages and step >= 2:
                scores(i + 1, step - 2)

    turn(-1, ("scores",))
    turn(0, ("soften", "scores"))

    def body(i, carry):
        turn(i, ("mix", "soften", "scores"))
        return carry

    lax.fori_loop(1, groups - 1, body, 0)
    turn(groups - 1, ("mix", "soften"))
    turn(groups, ("mix",))


def project_and_feed(x_ref, o_ref, g_ref, n_ref, out_w_ref, up_ref, down_ref, y_ref):
    block = x_ref.shape[0] // 2

    def half(i, carry):
        rows = pl.ds(pl.multiple_of(block * i, 256), block)
        y = x_ref[rows] + mm(o_ref[rows], out_w_ref[...])
        x_ref[rows] = y
        n_ref[rows] = norm(y)
        for p in range(4):
            lanes = slice(256 * p, 256 * p + 256)
            g_ref[:, lanes] = gelu2(mm(n_ref[rows], up_ref[:, lanes])).astype(BF16)
        y_ref[rows] = x_ref[rows] + 0.5 * mm(g_ref[...], down_ref[...])
        return carry

    half(0, 0)
    half(1, 0)


def local_kernel(
    first, strips,
    x_ref, above_ref, below_ref, left_ref, right_ref,
    table_ref, index_ref, *rest
):
    late, rest = rest[:7], rest[7:]
    res_ref, hid_ref, act_ref, xn_ref, sems = rest[:5]
    ew_ref, dw_ref, pw_ref, qkv_ref, out_w_ref, up_ref, down_ref, wt_ref = rest[5:13]
    bias_ref, xw_ref, n_ref, k_ref, qvt_ref, o_ref, g_ref, y_ref = rest[13:21]
    units = rest[21:]
    copies = fetch(late, rest[5:12], sems)
    rows = 8 * strips
    last = x_ref.shape[0]
    make_bias(table_ref, index_ref, bias_ref)

    for r in range(2):
        image = 8 * first + r - 1
        x = above_ref[0] if image < 0 else x_ref[image]
        xn_ref[64 * r : 64 * r + 64] = norm(x.astype(F32))
    for i, ref in enumerate((left_ref, right_ref)):
        xn_ref[128 + 64 * i : 128 + 64 * i + rows + 2] = norm(
            ref[8 * first : 8 * first + rows + 2].astype(F32)
        )

    def normalize(strip, carry):
        x = x_ref[pl.ds(8 * (first + strip) + 1, 8)].reshape(512, 256)
        xn_ref[pl.ds(pl.multiple_of(512 * strip + 256, 256), 512)] = norm(x.astype(F32))
        return carry

    ends = 8 * (first + strips) >= last
    lax.fori_loop(0, strips - 1 if ends else strips, normalize, 0)
    if ends:
        at = 512 * (strips - 1) + 256
        x = x_ref[last - 7 : last].reshape(448, 256)
        xn_ref[at : at + 448] = norm(x.astype(F32))
        xn_ref[at + 448 : at + 512] = norm(below_ref[0].astype(F32))

    def hidden_border(p):
        h = gelu2(mm(xn_ref[0:256], ew_ref[:, 256 * p : 256 * p + 256])).astype(F32)
        for c in range(2):
            lanes = slice(128 * c, 128 * c + 128)
            hid_ref[c, 0:2, 8:72, :] = h[0:128, lanes].reshape(2, 64, 128)
            for r in range(rows + 2):
                hid_ref[c, r, 7:8, :] = h[128 + r : 129 + r, lanes]
                hid_ref[c, r, 72:73, :] = h[192 + r : 193 + r, lanes]

    def hidden_part(p, part):
        at = pl.multiple_of(256 * strips * part + 256, 256)
        h = gelu2(mm(xn_ref[pl.ds(at, 256 * strips)], ew_ref[:, 256 * p : 256 * p + 256])).astype(F32)
        for c in range(2):
            lanes = slice(128 * c, 128 * c + 128)
            hid_ref[c, pl.ds(4 * strips * part + 2, 4 * strips), 8:72, :] = h[:, lanes].reshape(
                4 * strips, 64, 128
            )

    def conv_part(p, strip, c, half):
        w = (dw_ref[:, 256 * p + 128 * c : 256 * p + 128 * c + 128] * 0.5).astype(BF16)
        begin = 7 + 32 * half
        acc = [None] * 8
        for ir in range(10):
            h = [hid_ref[c, 8 * strip + ir, begin + d : begin + d + 32, :].astype(BF16) for d in range(3)]
            for dy in range(3):
                orow = ir - dy
                if 0 <= orow < 8:
                    t = h[0] * w[3 * dy : 3 * dy + 1] + h[1] * w[3 * dy + 1 : 3 * dy + 2]
                    t = t + h[2] * w[3 * dy + 2 : 3 * dy + 3]
                    acc[orow] = t if acc[orow] is None else acc[orow] + t
            if ir >= 2:
                to = pl.multiple_of(512 * strip + 64 * (ir - 2) + 32 * half, 32)
                lanes = slice(256 * p + 128 * c, 256 * p + 128 * c + 128)
                act_ref[pl.ds(to, 32), lanes] = gelu2(acc[ir - 2])

    for copy in copies[:2]:
        copy.wait()
    for p in range(4):
        hidden_border(p)

        def hidden(part, carry, p=p):
            hidden_part(p, part)
            return carry

        def conv(strip, carry, p=p):
            for c in range(2):
                for half in range(2):
                    conv_part(p, strip, c, half)
            return carry

        lax.fori_loop(0, 2, hidden, 0)
        lax.fori_loop(0, strips, conv, 0)

    def project(part, carry):
        at = pl.ds(pl.multiple_of(256 * strips * part, 256), 256 * strips)
        y_ref[at] = mm(act_ref[at], pw_ref[...])
        return carry

    def gather(strip, carry):
        at = pl.ds(pl.multiple_of(512 * strip, 512), 512)
        x = x_ref[pl.ds(8 * (first + strip), 8)].reshape(512, 256).astype(F32)
        y = (x + 0.5 * y_ref[at]).reshape(8, 64, 256)
        for w in range(8):
            to = pl.ds(pl.multiple_of(512 * strip + 64 * w, 64), 64)
            x = y[:, 8 * w : 8 * w + 8].reshape(64, 256)
            xw_ref[to] = x
            n_ref[to] = norm(x)
        return carry

    copies[2].wait()
    lax.fori_loop(0, 2, project, 0)
    lax.fori_loop(0, strips, gather, 0)
    copies[3].wait()
    for i in range(2):
        turned_map = qkv_ref[:, 512 * i : 512 * i + 256].astype(F32).T
        wt_ref[256 * i : 256 * i + 256] = turned_map.astype(BF16)
    attend(8 * strips, n_ref, qkv_ref, wt_ref, bias_ref, k_ref, qvt_ref, o_ref, units[:UNITS], units[UNITS : 2 * UNITS], units[2 * UNITS :])
    for copy in copies[4:]:
        copy.wait()
    project_and_feed(xw_ref, o_ref, g_ref, n_ref, out_w_ref, up_ref, down_ref, y_ref)

    def spread(strip, carry):
        for w in range(8):
            y = y_ref[pl.ds(pl.multiple_of(512 * strip + 64 * w, 64), 64)]
            res_ref[pl.ds(8 * strip, 8), 8 * w : 8 * w + 8, :] = y.reshape(8, 8, 256).astype(BF16)
        return carry

    lax.fori_loop(0, strips, spread, 0)


def grid_kernel(
    windows,
    x_ref, qkv_ref, wt_ref, table_ref, index_ref, late0_ref, late1_ref, late2_ref,
    res_ref,
    xs_ref, sems, out_w_ref, up_ref, down_ref, bias_ref, xw_ref, n_ref, k_ref, qvt_ref, o_ref, g_ref, y_ref, *units
):
    copies = fetch((late0_ref, late1_ref, late2_ref), (out_w_ref, up_ref, down_ref), sems)
    make_bias(table_ref, index_ref, bias_ref)
    x = x_ref[...].astype(F32).reshape(64 * windows, 256)
    xs_ref[0] = x[:, 0:128]
    xs_ref[1] = x[:, 128:256]
    for w in range(windows):
        rows = slice(64 * w, 64 * w + 64)
        for half in range(2):
            xw_ref[rows, 128 * half : 128 * half + 128] = xs_ref[half, pl.ds(w, 64, stride=windows), :]
    n_ref[...] = norm(xw_ref[...])
    attend(windows, n_ref, qkv_ref, wt_ref, bias_ref, k_ref, qvt_ref, o_ref, units[:UNITS], units[UNITS : 2 * UNITS], units[2 * UNITS :])
    for copy in copies:
        copy.wait()
    project_and_feed(xw_ref, o_ref, g_ref, n_ref, out_w_ref, up_ref, down_ref, y_ref)
    for w in range(windows):
        rows = slice(64 * w, 64 * w + 64)
        for half in range(2):
            xs_ref[half, pl.ds(w, 64, stride=windows), :] = y_ref[rows, 128 * half : 128 * half + 128]
    y = jnp.concatenate([xs_ref[0], xs_ref[1]], axis=1)
    res_ref[...] = y.reshape(64, windows, 256).astype(BF16)


UNIT_SCRATCH = (((128, 256), F32), ((128, 256), BF16), ((2, 256), F32))


def attend_scratch(windows):
    rows = 64 * windows
    return [
        pltpu.VMEM((2, 128, 256), F32),
        pltpu.VMEM((rows, 256), F32),
        pltpu.VMEM((rows, 256), BF16),
        pltpu.VMEM((rows, 256), BF16),
        pltpu.VMEM((512, rows), BF16),
        pltpu.VMEM((rows, 256), BF16),
        pltpu.VMEM((rows // 2, 1024), BF16),
        pltpu.VMEM((rows, 256), F32),
    ] + [pltpu.VMEM(shape, kind) for shape, kind in UNIT_SCRATCH for _ in range(UNITS)]


def on_chip(arrays):
    return tuple(pltpu.with_memory_space_constraint(a, pltpu.VMEM) for a in arrays)


def landing(arrays):
    return [pltpu.SemaphoreType.DMA((len(arrays),))] + [pltpu.VMEM(a.shape, a.dtype) for a in arrays]


def in_hbm(count):
    return [pl.BlockSpec(memory_space=pl.ANY)] * count


def in_vmem(count):
    return [pl.BlockSpec(memory_space=pltpu.VMEM)] * count


def local_stage(first, strips, cells, early, late):
    ops = tuple(cells) + tuple(early) + tuple(late)
    rows = 8 * strips
    return pl.pallas_call(
        functools.partial(local_kernel, first, strips),
        in_specs=in_vmem(len(cells) + len(early)) + in_hbm(len(late)),
        out_specs=in_vmem(1)[0],
        out_shape=jax.ShapeDtypeStruct((rows, 64, 256), BF16),
        scratch_shapes=[
            pltpu.VMEM((2, rows + 2, WIDE, 128), F32),
            pltpu.VMEM((64 * rows, 1024), BF16),
            pltpu.VMEM((64 * rows + 256, 256), BF16),
        ]
        + landing(late)
        + [pltpu.VMEM((512, 256), BF16)]
        + attend_scratch(8 * strips),
        compiler_params=PARAMS,
        name="local_stage",
    )(*ops)


def grid_stage(x, early, late):
    windows = x.shape[1]
    ops = (x,) + tuple(early) + tuple(late)
    return pl.pallas_call(
        functools.partial(grid_kernel, windows),
        in_specs=in_vmem(1 + len(early)) + in_hbm(len(late)),
        out_specs=in_vmem(1)[0],
        out_shape=jax.ShapeDtypeStruct(x.shape, BF16),
        scratch_shapes=[pltpu.VMEM((2, 64 * windows, 128), F32)] + landing(late) + attend_scratch(windows),
        compiler_params=PARAMS,
        name="grid_stage",
    )(*ops)


def bias_operands(table, index):
    turned_index = index.T
    return (
        jnp.pad(table.T, ((0, 0), (0, 256 - table.shape[0]))),
        jnp.concatenate([turned_index, turned_index], axis=1),
    )


def turned(qkv):
    return jnp.concatenate([qkv[:, :256], qkv[:, 512:]], axis=1).T


def neighbours(before, after, axes):
    count = lax.axis_size(axes)
    up = [(i, i + 1) for i in range(count - 1)]
    down = [(j, i) for i, j in up]
    return lax.ppermute(before, axes, up), lax.ppermute(after, axes, down)


def on_device(
    field, expand_w, dw_kernel, project_w,
    blk_qkv, blk_out, blk_table, blk_index, blk_up, blk_down,
    grid_qkv, grid_out, grid_table, grid_index, grid_up, grid_down,
):
    rows, cols, width = field.shape
    above, below = neighbours(field[-1:], field[:1], "ha")
    first = jnp.concatenate([above[:, 0], field[:, 0], below[:, 0]], axis=0)
    final = jnp.concatenate([above[:, -1], field[:, -1], below[:, -1]], axis=0)
    left, right = neighbours(final, first, ("wh", "core"))
    cells = (field,) + on_chip((above, below, left, right))
    local_w = bias_operands(blk_table, blk_index)
    local_late = (expand_w, dw_kernel, project_w, blk_qkv, blk_out, blk_up, blk_down)
    grid_w = (grid_qkv, turned(grid_qkv)) + bias_operands(grid_table, grid_index)
    grid_late = (grid_out, grid_up, grid_down)
    outs = []
    start = 0
    for strips in CHUNKS:
        part = local_stage(start, strips, cells, on_chip(local_w), local_late)
        start += strips
        part = part.reshape(64, strips * 8, width)
        moved = lax.all_to_all(part, ("ha", "wh"), 0, 0, tiled=True)
        (moved,) = on_chip((moved,))
        done = grid_stage(moved, on_chip(grid_w), grid_late)
        back = lax.all_to_all(done, ("ha", "wh"), 0, 0, tiled=True)
        outs.append(back.reshape(strips * 8, cols, width))
    return outs[0] if len(outs) == 1 else jnp.concatenate(outs, axis=0)


def solution(mesh):
    split = Mesh(mesh.devices.reshape(8, 8, 2), ("ha", "wh", "core"))
    spec = P("ha", ("wh", "core"), None)
    return jax.shard_map(
        on_device, mesh=split, in_specs=(spec,) + (P(),) * 15, out_specs=spec, check_vma=False
    )
```
